32 devices in a mesh: groups: 2 (over y), vocab: 4 (over z), req: 4 (over x, core).
Axes of the slice: x: 2, y: 2, z: 4, core: 2. Of those that a mesh axis runs over, the one named last changes fastest.
Arguments:
- last_states: bfloat16 [512, 8192], P('groups', 'req'), parts along dimension 0, may hold values from -300 to 300
- head_weight: bfloat16 [8192, 32000], P('req', 'vocab'), may hold values from -1 to 1
- embed_table: bfloat16 [32000, 8192], P('vocab', 'req'), may hold values from -200 to 200
- norm_gain: bfloat16 [8192], P('req'), may hold values from 0.099609375 to 1.8984375
- qkv_weight: bfloat16 [8192, 10240], P('req', 'vocab'), may hold values from -0.0625 to 0.0625
- active: int32 [512], P('groups'), parts along dimension 0, may hold values 0 or 1
- slot_request: int32 [512], P('groups'), parts along dimension 0, may hold values from 0 to 255, each once
Outputs:
- soft_embed: bfloat16 [512, 8192], P('groups', 'req'), parts along dimension 0
- qkv_out: bfloat16 [512, 10240], P(('groups', 'req'), 'vocab'), parts along dimension 0
The draws below stay inside these ranges and needn't reach their ends.
There are 2 independent parts, one for each index of `groups`. The reference program is written for one: setup_inputs(seed, part) draws one part's arguments, and reference() takes and returns one part's arrays. A program takes and returns all parts, laid end to end along the dimension named above; an argument that names none is the same for every part. Nothing has to cross between parts.
Inputs may be any that keep to these rules, and one draw needn't show every extreme that they name: `slot_request`: each slot serves a different request.
All inputs are finite; a program needn't handle non-finite values.
Results may differ from the reference program's by a relative error of at most 0.006.
Values may be sent and summed in bfloat16 or wider, within the bound.
A program may use at most 192 MiB of HBM per device.

```python
import math
import jax
import jax.numpy as jnp
from jax import lax

D = 8192
V = 32000
QKV = 10240
ROWS = 256


def draw_last_states(key, part):
    subkeys = jax.random.split(key, 2)
    row_scale = jnp.exp(jax.random.uniform(subkeys[0], (ROWS, 1), minval=math.log(18.0), maxval=math.log(48.0)))
    base = jnp.clip(jax.random.normal(subkeys[1], (ROWS, D)), -6.0, 6.0) * row_scale
    return base.astype(jnp.float32).astype(jnp.bfloat16)


def draw_head_weight(key, part):
    column = jnp.arange(V, dtype=jnp.float32)[None, :] / V
    index = jnp.arange(V)[None, :]
    rare = index >= V - V // 16
    factor = jnp.where(rare, 0.85, 0.6 + 0.8 * column)
    base = jnp.clip(jax.random.normal(key, (D, V)), -6.0, 6.0) * factor * 0.12 / math.sqrt(D)
    return base.astype(jnp.float32).astype(jnp.bfloat16)


def draw_embed_table(key, part):
    subkeys = jax.random.split(key, 5)
    row_scale = jnp.exp(jax.random.uniform(subkeys[0], (V, 1), minval=0.0, maxval=math.log(10.0)))
    position = jnp.arange(D, dtype=jnp.float32)[None, :] / D
    rare = jnp.arange(V)[:, None] >= V - V // 16
    col_scale = jnp.exp(jax.random.uniform(subkeys[1], (1, D), minval=0.0, maxval=math.log(10.0))) * 3.0 ** (0.5 * position)
    bulk = jnp.clip(jax.random.normal(subkeys[2], (V, D)), -6.0, 6.0) * row_scale * col_scale
    heavy = 60.0 * jnp.clip(jax.random.normal(subkeys[4], (V, D)), -3.2, 3.2)
    base = jnp.where(rare, heavy, 0.05 * bulk)
    return base.astype(jnp.float32).astype(jnp.bfloat16)


def place_ends(entries, key, smallest, high):
    extent = entries.shape
    place = [jax.random.randint(jax.random.fold_in(key, axis), (), 0, extent[axis]) for axis in range(len(extent))]
    entries = entries.at[tuple(place)].set(smallest)
    longest = extent.index(max(extent))
    place[longest] = (place[longest] + 1) % extent[longest]
    return entries.at[tuple(place)].set(high)


def block_levels(own_key, dims, cuts, least, high):
    loudness, own = 1.0, jax.random.fold_in(own_key, 6)
    for axis_at, blocks in cuts:
        steps = jnp.exp(jax.random.uniform(jax.random.fold_in(own, axis_at), (blocks,), jnp.float32, least / len(cuts), high / len(cuts)))
        loudness = loudness * jnp.repeat(steps, dims[axis_at] // blocks).reshape([-1 if axis == axis_at else 1 for axis in range(len(dims))])
    return loudness


def normal_values(own_key, dims, scale, bound, pieces=(), kind=jnp.bfloat16):
    level = block_levels(own_key, dims, pieces, -0.22, 0.18) if pieces else 1.0
    drawn = jax.random.normal(own_key, dims, jnp.float32) * scale * level
    return jnp.minimum(jnp.maximum(drawn, -bound), bound).astype(kind)


def setup_inputs(seed: int = 0, part: int = 0) -> dict:
    splits = jax.random.split(jax.random.key(seed), 8)
    part_splits = jax.random.split(jax.random.fold_in(splits[7], part), 8)
    last_states = draw_last_states(jax.random.fold_in(jax.random.fold_in(splits[7], part), 71), part)
    head_weight = draw_head_weight(jax.random.fold_in(splits[7], 71), part)
    embed_table = draw_embed_table(jax.random.fold_in(splits[7], 71), part)
    norm_gain = jnp.clip(1.0 + 0.18 * jax.random.normal(splits[3], (D,), jnp.float32), 0.099609375, 1.8984375).astype(jnp.bfloat16)
    qkv_weight = normal_values(splits[4], (D, QKV), D ** -0.5, 0.0625, ((0, 4), (1, 4)))
    active = place_ends((jax.random.randint(part_splits[5], (ROWS,), 0, 4) < 3).astype(jnp.int32), jax.random.fold_in(part_splits[5], 1), 0, 1)
    slot_request = jax.random.permutation(part_splits[6], ROWS).astype(jnp.int32)
    return dict(last_states=last_states, head_weight=head_weight, embed_table=embed_table, norm_gain=norm_gain, qkv_weight=qkv_weight, active=active, slot_request=slot_request)


def reference(last_states, head_weight, embed_table, norm_gain, qkv_weight, active, slot_request):
    slot_states = jnp.take(last_states, slot_request.astype(jnp.int32), axis=0)
    logits = jnp.dot(slot_states, head_weight, preferred_element_type=jnp.float32)
    row_top = lax.optimization_barrier(jnp.max(logits, axis=1, keepdims=True))
    shifted = jnp.exp(logits - row_top)
    row_total = lax.optimization_barrier(jnp.sum(shifted, axis=1, keepdims=True))
    weights = (shifted / row_total * active.astype(jnp.float32)[:, None]).astype(jnp.bfloat16)
    mixed = jnp.dot(weights, embed_table, preferred_element_type=jnp.float32)
    soft_embed = lax.optimization_barrier(mixed.astype(jnp.bfloat16))
    widened = soft_embed.astype(jnp.float32)
    inv_rms = lax.rsqrt(lax.optimization_barrier(jnp.mean(widened * widened, axis=1, keepdims=True)) + 1e-05)
    normed = (widened * inv_rms * norm_gain.astype(jnp.float32)[None, :]).astype(jnp.bfloat16)
    qkv_out = jnp.dot(normed, qkv_weight, preferred_element_type=jnp.float32).astype(jnp.bfloat16)
    return (soft_embed, qkv_out)
```

```python
import functools

import jax
import jax.numpy as jnp
from jax import lax
from jax.experimental import pallas as pl
from jax.experimental.pallas import tpu as pltpu
from jax.sharding import PartitionSpec as P

D = 8192
MESH = pl.DeviceIdType.MESH
VMEM_LIMIT = 56 * 1024 * 1024


def greet(targets):
    barrier = pltpu.get_barrier_semaphore()
    for target in targets:
        pl.semaphore_signal(barrier, inc=1, device_id=target, device_id_type=MESH)
    pl.semaphore_wait(barrier, len(targets))


def remote(src, dst, send, recv, target):
    return pltpu.make_async_remote_copy(
        src_ref=src, dst_ref=dst, send_sem=send, recv_sem=recv, device_id=target, device_id_type=MESH
    )


def req_position(nx):
    me = lax.axis_index("req")
    chip, core = lax.div(me, 2), lax.rem(me, 2)
    partner = {"req": chip * 2 + (1 - core)}

    def chip_at(d):
        return lax.rem(chip + d, nx)

    def peer(d):
        return {"req": chip_at(d) * 2 + core}

    return me, chip, core, partner, chip_at, peer


def vocab_peers(nz):
    z = lax.axis_index("vocab")
    return z, [{"vocab": lax.rem(z + d, nz)} for d in range(1, nz)]


def weights_kernel(nx, nz, steps, part_ref, active_ref, out_ref, core_buf, own_buf, chip_buf, stats,
                   stats_in, core_send, core_recv, own_sem, chip_send, chip_recv, stat_send, stat_recv,
                   pair_send, pair_recv, gather_send, gather_recv, fwd_send, fwd_recv):
    me, chip, core, partner, chip_at, peer = req_position(nx)
    _, zpeers = vocab_peers(nz)
    own_rows = part_ref.shape[0] // (2 * nx)
    s = own_rows // steps
    lane = lax.broadcasted_iota(jnp.int32, (s, 128), 1)
    greet([partner] + [peer(d) for d in range(1, nx)] + zpeers)

    core_copies, own_copies = [], []
    for j in range(steps):
        core_copies.append([])
        own_copies.append([])
        for d in list(range(1, nx)) + [0]:
            there = pl.multiple_of((chip_at(d) * 2 + 1 - core) * own_rows + j * s, s)
            here = pl.multiple_of((chip_at(d) * 2 + core) * own_rows + j * s, s)
            copy = remote(part_ref.at[pl.ds(there, s)], core_buf.at[j, d], core_send.at[j, d],
                          core_recv.at[j, d], partner)
            local = pltpu.make_async_copy(part_ref.at[pl.ds(here, s)], own_buf.at[j, d], own_sem.at[j, d])
            copy.start()
            local.start()
            core_copies[j].append(copy)
            own_copies[j].append(local)

    chip_copies, stat_copies, gather_copies, fwd_copies = {}, {}, {}, {}

    def reduce_cores(j):
        for i in range(nx):
            d = i + 1 if i < nx - 1 else 0
            own_copies[j][i].wait()
            core_copies[j][i].wait_recv()
            own_buf[j, d] = own_buf[j, d] + core_buf[j, d]
            if d > 0:
                copy = remote(own_buf.at[j, d], chip_buf.at[j, d - 1], chip_send.at[j, d - 1],
                              chip_recv.at[j, d - 1], peer(d))
                copy.start()
                chip_copies[j, d] = copy

    def exponentials(j):
        for d in range(1, nx):
            chip_copies[j, d].wait_recv()
        total = own_buf[j, 0]
        for d in range(1, nx):
            total = total + chip_buf[j, d - 1]
        top = jnp.max(total, axis=1, keepdims=True)
        shifted = jnp.exp(total - top)
        own_buf[j, 0] = shifted
        stats[j] = jnp.where(lane < 64, top, jnp.sum(shifted, axis=1, keepdims=True))
        for i, target in enumerate(zpeers):
            copy = remote(stats.at[j], stats_in.at[j, i], stat_send.at[j, i], stat_recv.at[j, i], target)
            copy.start()
            stat_copies[j, i] = copy

    def rows_of(owner, j):
        return pl.ds(pl.multiple_of(owner * own_rows + j * s, s), s)

    def normalise(j):
        for i in range(nz - 1):
            stat_copies[j, i].wait_recv()
        mine = stats[j]
        my_top, row_total = mine[:, 0:1], mine[:, 64:65]
        row_top = my_top
        for i in range(nz - 1):
            row_top = jnp.maximum(row_top, stats_in[j, i][:, 0:1])
        row_total = row_total * jnp.exp(my_top - row_top)
        for i in range(nz - 1):
            other = stats_in[j, i]
            row_total = row_total + other[:, 64:65] * jnp.exp(other[:, 0:1] - row_top)
        live = active_ref[rows_of(me, j), :][:, 0:1]
        factor = jnp.exp(my_top - row_top) / row_total * live
        mine_rows = out_ref.at[rows_of(me, j)]
        mine_rows[...] = (own_buf[j, 0] * factor).astype(out_ref.dtype)
        for d in range(1, nx):
            copy = remote(mine_rows, mine_rows, gather_send.at[j, d - 1], gather_recv.at[j, d - 1], peer(d))
            copy.start()
            gather_copies[j, d] = copy
        copy = remote(mine_rows, mine_rows, pair_send.at[j], pair_recv.at[j], partner)
        copy.start()
        gather_copies[j, 0] = copy

    def forward(j):
        for d in range(1, nx):
            gather_copies[j, d].wait_recv()
            block = out_ref.at[rows_of(chip_at(nx - d) * 2 + core, j)]
            copy = remote(block, block, fwd_send.at[j, d - 1], fwd_recv.at[j, d - 1], partner)
            copy.start()
            fwd_copies[j, d] = copy

    for t in range(steps + 3):
        if t < steps:
            reduce_cores(t)
        if 0 <= t - 1 < steps:
            exponentials(t - 1)
        if 0 <= t - 2 < steps:
            normalise(t - 2)
        if 0 <= t - 3 < steps:
            forward(t - 3)
    for j in range(steps):
        gather_copies[j, 0].wait_recv()
        for d in range(1, nx):
            fwd_copies[j, d].wait_recv()
    for j in range(steps):
        for copy in core_copies[j]:
            copy.wait_send()
    for group in (chip_copies, stat_copies, gather_copies, fwd_copies):
        for copy in group.values():
            copy.wait_send()


def gathered_weights(part, active, nx, nz):
    rows, words = part.shape
    steps = 4
    s = rows // (2 * nx) // steps
    far = max(nx - 1, 1)
    dma = pltpu.SemaphoreType.DMA
    return pl.pallas_call(
        functools.partial(weights_kernel, nx, nz, steps),
        out_shape=jax.ShapeDtypeStruct((rows, words), jnp.bfloat16),
        in_specs=[pl.BlockSpec(memory_space=pl.ANY), pl.BlockSpec(memory_space=pltpu.VMEM)],
        out_specs=pl.BlockSpec(memory_space=pltpu.VMEM),
        scratch_shapes=[
            pltpu.VMEM((steps, nx, s, words), jnp.float32),
            pltpu.VMEM((steps, nx, s, words), jnp.float32),
            pltpu.VMEM((steps, far, s, words), jnp.float32),
            pltpu.VMEM((steps, s, 128), jnp.float32),
            pltpu.VMEM((steps, nz - 1, s, 128), jnp.float32),
            dma((steps, nx)), dma((steps, nx)), dma((steps, nx)),
            dma((steps, far)), dma((steps, far)),
            dma((steps, nz - 1)), dma((steps, nz - 1)),
            dma((steps,)), dma((steps,)),
            dma((steps, far)), dma((steps, far)),
            dma((steps, far)), dma((steps, far)),
        ],
        compiler_params=pltpu.CompilerParams(
            collective_id=0, has_side_effects=True, vmem_limit_bytes=VMEM_LIMIT
        ),
        name="weights",
    )(part, active)


def embed_kernel(nz, parts, part_ref, out_ref, inbox, send, recv, out_send, out_recv):
    z, zpeers = vocab_peers(nz)
    rows = part_ref.shape[0] // nz
    s = rows // parts
    greet(zpeers)

    def rows_of(owner, h):
        return pl.ds(pl.multiple_of(owner * rows + h * s, s), s)

    copies, gathers = {}, {}
    for h in range(parts):
        for d in range(1, nz):
            copy = remote(part_ref.at[rows_of(lax.rem(z + d, nz), h)], inbox.at[h, d - 1],
                          send.at[h, d - 1], recv.at[h, d - 1], zpeers[d - 1])
            copy.start()
            copies[h, d] = copy
    for h in range(parts):
        total = part_ref[rows_of(z, h), :].astype(jnp.float32)
        for d in range(1, nz):
            copies[h, d].wait_recv()
            total = total + inbox[h, d - 1].astype(jnp.float32)
        block = out_ref.at[rows_of(z, h)]
        block[...] = total.astype(out_ref.dtype)
        for d in range(1, nz):
            copy = remote(block, block, out_send.at[h, d - 1], out_recv.at[h, d - 1], zpeers[d - 1])
            copy.start()
            gathers[h, d] = copy
    for copy in gathers.values():
        copy.wait_recv()
    for copy in list(copies.values()) + list(gathers.values()):
        copy.wait_send()


def summed_embed(part, nz):
    rows, columns = part.shape
    parts = 2
    s = rows // nz // parts
    dma = pltpu.SemaphoreType.DMA
    return pl.pallas_call(
        functools.partial(embed_kernel, nz, parts),
        out_shape=jax.ShapeDtypeStruct((rows, columns), jnp.bfloat16),
        in_specs=[pl.BlockSpec(memory_space=pltpu.VMEM)],
        out_specs=pl.BlockSpec(memory_space=pltpu.VMEM),
        scratch_shapes=[
            pltpu.VMEM((parts, nz - 1, s, columns), jnp.bfloat16),
            dma((parts, nz - 1)), dma((parts, nz - 1)), dma((parts, nz - 1)), dma((parts, nz - 1)),
        ],
        compiler_params=pltpu.CompilerParams(
            collective_id=1, has_side_effects=True, vmem_limit_bytes=VMEM_LIMIT
        ),
        name="embed_sum",
    )(part)


def qkv_kernel(nx, steps, part_ref, squares_ref, out_ref, core_buf, own_buf, chip_out, chip_in, squares_in,
               core_send, core_recv, own_sem, chip_send, chip_recv, sq_send, sq_recv):
    me, chip, core, partner, chip_at, peer = req_position(nx)
    own_rows = part_ref.shape[0] // (2 * nx)
    s = own_rows // steps
    n = 2 * nx
    others = [lax.rem(me + d, n) for d in range(1, n)]
    greet([{"req": other} for other in others])

    core_copies, own_copies = [], []
    for j in range(steps):
        core_copies.append([])
        own_copies.append([])
        for d in list(range(1, nx)) + [0]:
            there = pl.multiple_of((chip_at(d) * 2 + 1 - core) * own_rows + j * s, s)
            here = pl.multiple_of((chip_at(d) * 2 + core) * own_rows + j * s, s)
            copy = remote(part_ref.at[pl.ds(there, s)], core_buf.at[j, d], core_send.at[j, d],
                          core_recv.at[j, d], partner)
            local = pltpu.make_async_copy(part_ref.at[pl.ds(here, s)], own_buf.at[j, d], own_sem.at[j, d])
            copy.start()
            local.start()
            core_copies[j].append(copy)
            own_copies[j].append(local)
    sq_copies = []
    for i, other in enumerate(others):
        block = squares_ref.at[pl.ds(pl.multiple_of(other * own_rows, own_rows), own_rows)]
        copy = remote(block, squares_in.at[i], sq_send.at[i], sq_recv.at[i], {"req": other})
        copy.start()
        sq_copies.append(copy)

    chip_copies = {}
    for j in range(steps):
        for i in range(nx):
            d = i + 1 if i < nx - 1 else 0
            own_copies[j][i].wait()
            core_copies[j][i].wait_recv()
            total = own_buf[j, d] + core_buf[j, d]
            if d > 0:
                chip_out[j, d - 1] = total.astype(chip_out.dtype)
                copy = remote(chip_out.at[j, d - 1], chip_in.at[j, d - 1], chip_send.at[j, d - 1],
                              chip_recv.at[j, d - 1], peer(d))
                copy.start()
                chip_copies[j, d] = copy
            else:
                own_buf[j, 0] = total
    squares = squares_ref[pl.ds(pl.multiple_of(me * own_rows, own_rows), own_rows), :]
    for i, copy in enumerate(sq_copies):
        copy.wait_recv()
        squares = squares + squares_in[i]
    inv_rms = lax.rsqrt(squares[:, 0:1] / D + 1e-05)
    for j in range(steps):
        total = own_buf[j, 0]
        for d in range(1, nx):
            chip_copies[j, d].wait_recv()
            total = total + chip_in[j, d - 1].astype(jnp.float32)
        out_ref[j * s : (j + 1) * s, :] = (total * inv_rms[j * s : (j + 1) * s]).astype(out_ref.dtype)
    for j in range(steps):
        for copy in core_copies[j]:
            copy.wait_send()
    for copy in sq_copies + list(chip_copies.values()):
        copy.wait_send()


def scattered_qkv(part, squares, nx):
    rows, columns = part.shape
    steps = 2
    own = rows // (2 * nx)
    s = own // steps
    far = max(nx - 1, 1)
    dma = pltpu.SemaphoreType.DMA
    return pl.pallas_call(
        functools.partial(qkv_kernel, nx, steps),
        out_shape=jax.ShapeDtypeStruct((own, columns), jnp.bfloat16),
        in_specs=[pl.BlockSpec(memory_space=pl.ANY), pl.BlockSpec(memory_space=pltpu.VMEM)],
        out_specs=pl.BlockSpec(memory_space=pltpu.VMEM),
        scratch_shapes=[
            pltpu.VMEM((steps, nx, s, columns), jnp.float32),
            pltpu.VMEM((steps, nx, s, columns), jnp.float32),
            pltpu.VMEM((steps, far, s, columns), jnp.bfloat16),
            pltpu.VMEM((steps, far, s, columns), jnp.bfloat16),
            pltpu.VMEM((2 * nx - 1, own, 128), jnp.float32),
            dma((steps, nx)), dma((steps, nx)), dma((steps, nx)),
            dma((steps, far)), dma((steps, far)),
            dma((2 * nx - 1,)), dma((2 * nx - 1,)),
        ],
        compiler_params=pltpu.CompilerParams(
            collective_id=2, has_side_effects=True, vmem_limit_bytes=VMEM_LIMIT
        ),
        name="qkv_sum",
    )(part, squares)


def on_device(nx, nz, last_states, head_weight, embed_table, norm_gain, qkv_weight, active, slot_request):
    rows = last_states.shape[0]
    state_rows = jnp.take(last_states, slot_request, axis=0)
    partial_logits = jnp.dot(state_rows, head_weight, preferred_element_type=jnp.float32)
    live = jnp.broadcast_to(active.astype(jnp.float32)[:, None], (rows, 128))
    weights = gathered_weights(partial_logits, live, nx, nz)
    partial_embed = jnp.dot(weights, embed_table, preferred_element_type=jnp.float32)
    soft_embed = summed_embed(partial_embed.astype(jnp.bfloat16), nz)
    widened = soft_embed.astype(jnp.float32)
    squares = jnp.broadcast_to(jnp.sum(widened * widened, axis=1)[:, None], (rows, 128))
    scaled = (widened * norm_gain.astype(jnp.float32)[None, :]).astype(jnp.bfloat16)
    partial_qkv = jnp.dot(scaled, qkv_weight, preferred_element_type=jnp.float32)
    return (soft_embed, scattered_qkv(partial_qkv, squares, nx))


def solution(mesh):
    nx, nz = mesh.shape["req"] // 2, mesh.shape["vocab"]
    return jax.shard_map(
        functools.partial(on_device, nx, nz),
        mesh=mesh,
        in_specs=(
            P("groups", "req"),
            P("req", "vocab"),
            P("vocab", "req"),
            P("req"),
            P("req", "vocab"),
            P("groups"),
            P("groups"),
        ),
        out_specs=(P("groups", "req"), P(("groups", "req"), "vocab")),
        check_vma=False,
    )
```

```python
import functools

import jax
import jax.numpy as jnp
from jax import lax
from jax.experimental import pallas as pl
from jax.experimental.pallas import tpu as pltpu
from jax.sharding import PartitionSpec as P

D = 8192
MESH = pl.DeviceIdType.MESH
VMEM_LIMIT = 60 * 1024 * 1024


def greet(targets):
    barrier = pltpu.get_barrier_semaphore()
    for target in targets:
        pl.semaphore_signal(barrier, inc=1, device_id=target, device_id_type=MESH)
    pl.semaphore_wait(barrier, len(targets))


def remote(src, dst, send, recv, target):
    return pltpu.make_async_remote_copy(
        src_ref=src, dst_ref=dst, send_sem=send, recv_sem=recv, device_id=target, device_id_type=MESH
    )


def req_position(nx):
    me = lax.axis_index("req")
    chip, core = lax.div(me, 2), lax.rem(me, 2)
    partner = {"req": chip * 2 + (1 - core)}

    def chip_at(d):
        return lax.rem(chip + d, nx)

    def peer(d):
        return {"req": chip_at(d) * 2 + core}

    return me, chip, core, partner, chip_at, peer


def vocab_peers(nz):
    z = lax.axis_index("vocab")
    return z, [{"vocab": lax.rem(z + d, nz)} for d in range(1, nz)]


def mixed_kernel(nx, nz, steps, part_ref, active_ref, embed_ref, out_ref, core_buf, own_buf, chip_buf,
                 weights, table, mixed, inbox, stats, stats_in, table_sem, core_send, core_recv, own_sem,
                 chip_send, chip_recv, stat_send, stat_recv, pair_send, pair_recv, gather_send,
                 gather_recv, fwd_send, fwd_recv, mix_send, mix_recv, out_send, out_recv):
    me, chip, core, partner, chip_at, peer = req_position(nx)
    z, zpeers = vocab_peers(nz)
    own_rows = part_ref.shape[0] // (2 * nx)
    s = own_rows // steps
    piece = 2 * nx * s // nz
    tile = 256
    lane = lax.broadcasted_iota(jnp.int32, (s, 128), 1)
    greet([partner] + [peer(d) for d in range(1, nx)] + zpeers)

    core_copies, own_copies = [], []
    for j in range(steps):
        core_copies.append([])
        own_copies.append([])
        for d in list(range(1, nx)) + [0]:
            there = pl.multiple_of((chip_at(d) * 2 + 1 - core) * own_rows + j * s, s)
            here = pl.multiple_of((chip_at(d) * 2 + core) * own_rows + j * s, s)
            copy = remote(part_ref.at[pl.ds(there, s)], core_buf.at[j, d], core_send.at[j, d],
                          core_recv.at[j, d], partner)
            local = pltpu.make_async_copy(part_ref.at[pl.ds(here, s)], own_buf.at[j, d], own_sem.at[j, d])
            copy.start()
            local.start()
            core_copies[j].append(copy)
            own_copies[j].append(local)
    table_copy = pltpu.make_async_copy(embed_ref, table, table_sem)
    table_copy.start()

    chip_copies, stat_copies, gather_copies, fwd_copies = {}, {}, {}, {}
    mix_copies, out_copies = {}, {}

    def reduce_cores(j):
        for i in range(nx):
            d = i + 1 if i < nx - 1 else 0
            own_copies[j][i].wait()
            core_copies[j][i].wait_recv()
            own_buf[j, d] = own_buf[j, d] + core_buf[j, d]
            if d > 0:
                copy = remote(own_buf.at[j, d], chip_buf.at[j, d - 1], chip_send.at[j, d - 1],
                              chip_recv.at[j, d - 1], peer(d))
                copy.start()
                chip_copies[j, d] = copy

    def exponentials(j):
        for d in range(1, nx):
            chip_copies[j, d].wait_recv()
        total = own_buf[j, 0]
        for d in range(1, nx):
            total = total + chip_buf[j, d - 1]
        top = jnp.max(total, axis=1, keepdims=True)
        shifted = jnp.exp(total - top)
        own_buf[j, 0] = shifted
        stats[j] = jnp.where(lane < 64, top, jnp.sum(shifted, axis=1, keepdims=True))
        for i, target in enumerate(zpeers):
            copy = remote(stats.at[j], stats_in.at[j, i], stat_send.at[j, i], stat_recv.at[j, i], target)
            copy.start()
            stat_copies[j, i] = copy

    def rows_of(owner):
        return pl.ds(pl.multiple_of(owner * s, s), s)

    def normalise(j):
        for i in range(nz - 1):
            stat_copies[j, i].wait_recv()
        mine = stats[j]
        my_top, row_total = mine[:, 0:1], mine[:, 64:65]
        row_top = my_top
        for i in range(nz - 1):
            row_top = jnp.maximum(row_top, stats_in[j, i][:, 0:1])
        row_total = row_total * jnp.exp(my_top - row_top)
        for i in range(nz - 1):
            other = stats_in[j, i]
            row_total = row_total + other[:, 64:65] * jnp.exp(other[:, 0:1] - row_top)
        live = active_ref[pl.ds(pl.multiple_of(me * own_rows + j * s, s), s), :][:, 0:1]
        factor = jnp.exp(my_top - row_top) / row_total * live
        mine_rows = weights.at[j, rows_of(me)]
        mine_rows[...] = (own_buf[j, 0] * factor).astype(weights.dtype)
        for d in range(1, nx):
            copy = remote(mine_rows, mine_rows, gather_send.at[j, d - 1], gather_recv.at[j, d - 1], peer(d))
            copy.start()
            gather_copies[j, d] = copy
        copy = remote(mine_rows, mine_rows, pair_send.at[j], pair_recv.at[j], partner)
        copy.start()
        gather_copies[j, 0] = copy

    def forward(j):
        for d in range(1, nx):
            gather_copies[j, d].wait_recv()
            block = weights.at[j, rows_of(chip_at(nx - d) * 2 + core)]
            copy = remote(block, block, fwd_send.at[j, d - 1], fwd_recv.at[j, d - 1], partner)
            copy.start()
            fwd_copies[j, d] = copy

    def piece_of(owner):
        return pl.ds(pl.multiple_of(owner * piece, piece), piece)

    def mix(j):
        if j == 0:
            table_copy.wait()
        gather_copies[j, 0].wait_recv()
        for d in range(1, nx):
            fwd_copies[j, d].wait_recv()

        @pl.loop(0, table.shape[1] // tile)
        def _(c):
            columns = pl.ds(pl.multiple_of(c * tile, tile), tile)
            mixed[j, :, columns] = jnp.dot(
                weights[j], table[:, columns], preferred_element_type=jnp.float32
            ).astype(mixed.dtype)

        for d in range(1, nz):
            copy = remote(mixed.at[j, piece_of(lax.rem(z + d, nz))], inbox.at[j, d - 1],
                          mix_send.at[j, d - 1], mix_recv.at[j, d - 1], zpeers[d - 1])
            copy.start()
            mix_copies[j, d] = copy

    def gather_mixed(j):
        total = mixed[j, piece_of(z), :].astype(jnp.float32)
        for d in range(1, nz):
            mix_copies[j, d].wait_recv()
            total = total + inbox[j, d - 1].astype(jnp.float32)
        block = out_ref.at[j, piece_of(z)]
        block[...] = total.astype(out_ref.dtype)
        for d in range(1, nz):
            copy = remote(block, block, out_send.at[j, d - 1], out_recv.at[j, d - 1], zpeers[d - 1])
            copy.start()
            out_copies[j, d] = copy

    for t in range(min(2, steps)):
        reduce_cores(t)
    for t in range(steps):
        exponentials(t)
        if t >= 2:
            gather_mixed(t - 2)
        normalise(t)
        if t + 2 < steps:
            reduce_cores(t + 2)
        if t >= 1:
            forward(t - 1)
            mix(t - 1)
    if steps >= 2:
        gather_mixed(steps - 2)
    forward(steps - 1)
    mix(steps - 1)
    gather_mixed(steps - 1)
    for copy in out_copies.values():
        copy.wait_recv()
    for j in range(steps):
        for copy in core_copies[j]:
            copy.wait_send()
    for group in (chip_copies, stat_copies, gather_copies, fwd_copies, mix_copies, out_copies):
        for copy in group.values():
            copy.wait_send()


def expected_embedding(part, active, embed_table, nx, nz, steps):
    rows, words = part.shape
    width = embed_table.shape[1]
    s = rows // (2 * nx) // steps
    block = 2 * nx * s
    far = max(nx - 1, 1)
    dma = pltpu.SemaphoreType.DMA
    return pl.pallas_call(
        functools.partial(mixed_kernel, nx, nz, steps),
        out_shape=jax.ShapeDtypeStruct((steps, block, width), jnp.bfloat16),
        in_specs=[
            pl.BlockSpec(memory_space=pl.ANY),
            pl.BlockSpec(memory_space=pltpu.VMEM),
            pl.BlockSpec(memory_space=pl.ANY),
        ],
        out_specs=pl.BlockSpec(memory_space=pltpu.VMEM),
        scratch_shapes=[
            pltpu.VMEM((steps, nx, s, words), jnp.float32),
            pltpu.VMEM((steps, nx, s, words), jnp.float32),
            pltpu.VMEM((steps, far, s, words), jnp.float32),
            pltpu.VMEM((steps, block, words), jnp.bfloat16),
            pltpu.VMEM((words, width), jnp.bfloat16),
            pltpu.VMEM((steps, block, width), jnp.bfloat16),
            pltpu.VMEM((steps, nz - 1, block // nz, width), jnp.bfloat16),
            pltpu.VMEM((steps, s, 128), jnp.float32),
            pltpu.VMEM((steps, nz - 1, s, 128), jnp.float32),
            dma,
            dma((steps, nx)), dma((steps, nx)), dma((steps, nx)),
            dma((steps, far)), dma((steps, far)),
            dma((steps, nz - 1)), dma((steps, nz - 1)),
            dma((steps,)), dma((steps,)),
            dma((steps, far)), dma((steps, far)),
            dma((steps, far)), dma((steps, far)),
            dma((steps, nz - 1)), dma((steps, nz - 1)),
            dma((steps, nz - 1)), dma((steps, nz - 1)),
        ],
        compiler_params=pltpu.CompilerParams(
            collective_id=0, has_side_effects=True, vmem_limit_bytes=VMEM_LIMIT
        ),
        name="expected_embedding",
    )(part, active, embed_table)


def qkv_kernel(nx, steps, part_ref, squares_ref, out_ref, core_buf, own_buf, chip_out, chip_in, squares_in,
               core_send, core_recv, own_sem, chip_send, chip_recv, sq_send, sq_recv):
    me, chip, core, partner, chip_at, peer = req_position(nx)
    own_rows = part_ref.shape[0] // (2 * nx)
    s = own_rows // steps
    n = 2 * nx
    others = [lax.rem(me + d, n) for d in range(1, n)]
    greet([{"req": other} for other in others])

    core_copies, own_copies = [], []
    for j in range(steps):
        core_copies.append([])
        own_copies.append([])
        for d in list(range(1, nx)) + [0]:
            there = pl.multiple_of(j * n * s + (chip_at(d) * 2 + 1 - core) * s, s)
            here = pl.multiple_of(j * n * s + (chip_at(d) * 2 + core) * s, s)
            copy = remote(part_ref.at[pl.ds(there, s)], core_buf.at[j, d], core_send.at[j, d],
                          core_recv.at[j, d], partner)
            local = pltpu.make_async_copy(part_ref.at[pl.ds(here, s)], own_buf.at[j, d], own_sem.at[j, d])
            copy.start()
            local.start()
            core_copies[j].append(copy)
            own_copies[j].append(local)
    sq_copies = []
    for i, other in enumerate(others):
        block = squares_ref.at[:, other]
        copy = remote(block, squares_in.at[i], sq_send.at[i], sq_recv.at[i], {"req": other})
        copy.start()
        sq_copies.append(copy)

    chip_copies = {}
    for j in range(steps):
        for i in range(nx):
            d = i + 1 if i < nx - 1 else 0
            own_copies[j][i].wait()
            core_copies[j][i].wait_recv()
            total = own_buf[j, d] + core_buf[j, d]
            if d > 0:
                chip_out[j, d - 1] = total.astype(chip_out.dtype)
                copy = remote(chip_out.at[j, d - 1], chip_in.at[j, d - 1], chip_send.at[j, d - 1],
                              chip_recv.at[j, d - 1], peer(d))
                copy.start()
                chip_copies[j, d] = copy
            else:
                own_buf[j, 0] = total
    squares = squares_ref[:, me]
    for i, copy in enumerate(sq_copies):
        copy.wait_recv()
        squares = squares + squares_in[i]
    inv_rms = lax.rsqrt(squares[:, :, 0:1] / D + 1e-05)
    for j in range(steps):
        total = own_buf[j, 0]
        for d in range(1, nx):
            chip_copies[j, d].wait_recv()
            total = total + chip_in[j, d - 1].astype(jnp.float32)
        out_ref[j * s : (j + 1) * s, :] = (total * inv_rms[j]).astype(out_ref.dtype)
    for j in range(steps):
        for copy in core_copies[j]:
            copy.wait_send()
    for copy in sq_copies + list(chip_copies.values()):
        copy.wait_send()


def scattered_qkv(part, squares, nx):
    rows, columns = part.shape
    steps = squares.shape[0]
    own = rows // (2 * nx)
    s = own // steps
    far = max(nx - 1, 1)
    dma = pltpu.SemaphoreType.DMA
    return pl.pallas_call(
        functools.partial(qkv_kernel, nx, steps),
        out_shape=jax.ShapeDtypeStruct((own, columns), jnp.bfloat16),
        in_specs=[pl.BlockSpec(memory_space=pl.ANY), pl.BlockSpec(memory_space=pltpu.VMEM)],
        out_specs=pl.BlockSpec(memory_space=pltpu.VMEM),
        scratch_shapes=[
            pltpu.VMEM((steps, nx, s, columns), jnp.float32),
            pltpu.VMEM((steps, nx, s, columns), jnp.float32),
            pltpu.VMEM((steps, far, s, columns), jnp.bfloat16),
            pltpu.VMEM((steps, far, s, columns), jnp.bfloat16),
            pltpu.VMEM((2 * nx - 1, steps, s, 128), jnp.float32),
            dma((steps, nx)), dma((steps, nx)), dma((steps, nx)),
            dma((steps, far)), dma((steps, far)),
            dma((2 * nx - 1,)), dma((2 * nx - 1,)),
        ],
        compiler_params=pltpu.CompilerParams(
            collective_id=2, has_side_effects=True, vmem_limit_bytes=VMEM_LIMIT
        ),
        name="qkv_sum",
    )(part, squares)


def on_device(nx, nz, last_states, head_weight, embed_table, norm_gain, qkv_weight, active, slot_request):
    rows = last_states.shape[0]
    state_rows = jnp.take(last_states, slot_request, axis=0)
    partial_logits = jnp.dot(state_rows, head_weight, preferred_element_type=jnp.float32)
    live = jnp.broadcast_to(active.astype(jnp.float32)[:, None], (rows, 128))
    own_rows = rows // (2 * nx)
    steps = 4
    while steps > 1 and (rows // steps // nz) % 16:
        steps //= 2
    s = own_rows // steps
    blocks = expected_embedding(partial_logits, live, embed_table, nx, nz, steps)
    widened = blocks.reshape(rows, -1).astype(jnp.float32)
    squares = jnp.broadcast_to(jnp.sum(widened * widened, axis=1)[:, None], (rows, 128))
    scaled = (widened * norm_gain.astype(jnp.float32)[None, :]).astype(jnp.bfloat16)
    partial_qkv = jnp.dot(scaled, qkv_weight, preferred_element_type=jnp.float32)
    qkv_out = scattered_qkv(partial_qkv, squares.reshape(steps, 2 * nx, s, 128), nx)
    soft_embed = blocks.reshape(steps, 2 * nx, s, -1).transpose(1, 0, 2, 3).reshape(rows, -1)
    return (soft_embed, qkv_out)


def solution(mesh):
    nx, nz = mesh.shape["req"] // 2, mesh.shape["vocab"]
    return jax.shard_map(
        functools.partial(on_device, nx, nz),
        mesh=mesh,
        in_specs=(
            P("groups", "req"),
            P("req", "vocab"),
            P("vocab", "req"),
            P("req"),
            P("req", "vocab"),
            P("groups"),
            P("groups"),
        ),
        out_specs=(P("groups", "req"), P(("groups", "req"), "vocab")),
        check_vma=False,
    )
```

```python
import functools

import jax
import jax.numpy as jnp
from jax import lax
from jax.experimental import pallas as pl
from jax.experimental.pallas import tpu as pltpu
from jax.sharding import PartitionSpec as P

D = 8192
MESH = pl.DeviceIdType.MESH
VMEM_LIMIT = 60 * 1024 * 1024


def greet(targets):
    barrier = pltpu.get_barrier_semaphore()
    for target in targets:
        pl.semaphore_signal(barrier, inc=1, device_id=target, device_id_type=MESH)
    pl.semaphore_wait(barrier, len(targets))


def remote(src, dst, send, recv, target):
    return pltpu.make_async_remote_copy(
        src_ref=src, dst_ref=dst, send_sem=send, recv_sem=recv, device_id=target, device_id_type=MESH
    )


def req_position(nx):
    me = lax.axis_index("req")
    chip, core = lax.div(me, 2), lax.rem(me, 2)
    partner = {"req": chip * 2 + (1 - core)}

    def chip_at(d):
        return lax.rem(chip + d, nx)

    def peer(d):
        return {"req": chip_at(d) * 2 + core}

    return me, chip, core, partner, chip_at, peer


def vocab_peers(nz):
    z = lax.axis_index("vocab")
    return z, [{"vocab": lax.rem(z + d, nz)} for d in range(1, nz)]


def mixed_kernel(nx, nz, steps, part_ref, active_ref, embed_ref, out_ref, core_buf, own_buf, chip_buf,
                 weights, table, mixed, inbox, stats, stats_in, table_sem, core_send, core_recv, own_sem,
                 chip_send, chip_recv, stat_send, stat_recv, pair_send, pair_recv, gather_send,
                 gather_recv, fwd_send, fwd_recv, mix_send, mix_recv, out_send, out_recv):
    me, chip, core, partner, chip_at, peer = req_position(nx)
    z, zpeers = vocab_peers(nz)
    own_rows = part_ref.shape[0] // (2 * nx)
    s = own_rows // steps
    piece = 2 * nx * s // nz
    halves = 2
    half = table.shape[1] // halves
    tile = min(512, half)
    lane = lax.broadcasted_iota(jnp.int32, (s, 128), 1)
    greet([partner] + [peer(d) for d in range(1, nx)] + zpeers)

    core_copies, own_copies = [], []
    for j in range(steps):
        core_copies.append([])
        own_copies.append([])
        for d in list(range(1, nx)) + [0]:
            there = pl.multiple_of((chip_at(d) * 2 + 1 - core) * own_rows + j * s, s)
            here = pl.multiple_of((chip_at(d) * 2 + core) * own_rows + j * s, s)
            copy = remote(part_ref.at[pl.ds(there, s)], core_buf.at[j, d], core_send.at[j, d],
                          core_recv.at[j, d], partner)
            local = pltpu.make_async_copy(part_ref.at[pl.ds(here, s)], own_buf.at[j, d], own_sem.at[j, d])
            copy.start()
            local.start()
            core_copies[j].append(copy)
            own_copies[j].append(local)
    table_copy = pltpu.make_async_copy(embed_ref, table, table_sem)
    table_copy.start()

    chip_copies, stat_copies, gather_copies, fwd_copies = {}, {}, {}, {}
    mix_copies, out_copies = {}, {}

    def reduce_cores(j):
        for i in range(nx):
            d = i + 1 if i < nx - 1 else 0
            own_copies[j][i].wait()
            core_copies[j][i].wait_recv()
            own_buf[j, d] = own_buf[j, d] + core_buf[j, d]
            if d > 0:
                copy = remote(own_buf.at[j, d], chip_buf.at[j, d - 1], chip_send.at[j, d - 1],
                              chip_recv.at[j, d - 1], peer(d))
                copy.start()
                chip_copies[j, d] = copy

    def exponentials(j):
        for d in range(1, nx):
            chip_copies[j, d].wait_recv()
        total = own_buf[j, 0]
        for d in range(1, nx):
            total = total + chip_buf[j, d - 1]
        top = jnp.max(total, axis=1, keepdims=True)
        shifted = jnp.exp(total - top)
        own_buf[j, 0] = shifted
        stats[j] = jnp.where(lane < 64, top, jnp.sum(shifted, axis=1, keepdims=True))
        for i, target in enumerate(zpeers):
            copy = remote(stats.at[j], stats_in.at[j, i], stat_send.at[j, i], stat_recv.at[j, i], target)
            copy.start()
            stat_copies[j, i] = copy

    def rows_of(owner):
        return pl.ds(pl.multiple_of(owner * s, s), s)

    def normalise(j):
        for i in range(nz - 1):
            stat_copies[j, i].wait_recv()
        mine = stats[j]
        my_top, row_total = mine[:, 0:1], mine[:, 64:65]
        row_top = my_top
        for i in range(nz - 1):
            row_top = jnp.maximum(row_top, stats_in[j, i][:, 0:1])
        row_total = row_total * jnp.exp(my_top - row_top)
        for i in range(nz - 1):
            other = stats_in[j, i]
            row_total = row_total + other[:, 64:65] * jnp.exp(other[:, 0:1] - row_top)
        live = active_ref[pl.ds(pl.multiple_of(me * own_rows + j * s, s), s), :][:, 0:1]
        factor = jnp.exp(my_top - row_top) / row_total * live
        mine_rows = weights.at[j, rows_of(me)]
        mine_rows[...] = (own_buf[j, 0] * factor).astype(weights.dtype)
        for d in range(1, nx):
            copy = remote(mine_rows, mine_rows, gather_send.at[j, d - 1], gather_recv.at[j, d - 1], peer(d))
            copy.start()
            gather_copies[j, d] = copy
        copy = remote(mine_rows, mine_rows, pair_send.at[j], pair_recv.at[j], partner)
        copy.start()
        gather_copies[j, 0] = copy

    def forward(j):
        for d in range(1, nx):
            gather_copies[j, d].wait_recv()
            block = weights.at[j, rows_of(chip_at(nx - d) * 2 + core)]
            copy = remote(block, block, fwd_send.at[j, d - 1], fwd_recv.at[j, d - 1], partner)
            copy.start()
            fwd_copies[j, d] = copy

    def piece_of(owner):
        return pl.ds(pl.multiple_of(owner * piece, piece), piece)

    def mix(j):
        if j == 0:
            table_copy.wait()
        gather_copies[j, 0].wait_recv()
        for d in range(1, nx):
            fwd_copies[j, d].wait_recv()

        for h in range(halves):

            @pl.loop(h * half // tile, (h + 1) * half // tile)
            def _(c):
                columns = pl.ds(pl.multiple_of(c * tile, tile), tile)
                mixed[j, :, columns] = jnp.dot(
                    weights[j], table[:, columns], preferred_element_type=jnp.float32
                ).astype(mixed.dtype)

            columns = pl.ds(h * half, half)
            for d in range(1, nz):
                copy = remote(mixed.at[j, piece_of(lax.rem(z + d, nz)), columns],
                              inbox.at[j, d - 1, :, columns],
                              mix_send.at[j, h, d - 1], mix_recv.at[j, h, d - 1], zpeers[d - 1])
                copy.start()
                mix_copies[j, h, d] = copy

    def gather_mixed(j):
        for h in range(halves):
            columns = pl.ds(h * half, half)
            total = mixed[j, piece_of(z), columns].astype(jnp.float32)
            for d in range(1, nz):
                mix_copies[j, h, d].wait_recv()
                total = total + inbox[j, d - 1, :, columns].astype(jnp.float32)
            block = out_ref.at[j, piece_of(z), columns]
            block[...] = total.astype(out_ref.dtype)
            for d in range(1, nz):
                copy = remote(block, block, out_send.at[j, h, d - 1], out_recv.at[j, h, d - 1],
                              zpeers[d - 1])
                copy.start()
                out_copies[j, h, d] = copy

    for t in range(min(2, steps)):
        reduce_cores(t)
    for t in range(steps):
        exponentials(t)
        if t >= 2:
            gather_mixed(t - 2)
        normalise(t)
        if t + 2 < steps:
            reduce_cores(t + 2)
        if t >= 1:
            forward(t - 1)
            mix(t - 1)
    forward(steps - 1)
    if steps >= 2:
        gather_mixed(steps - 2)
    mix(steps - 1)
    gather_mixed(steps - 1)
    for copy in out_copies.values():
        copy.wait_recv()
    for j in range(steps):
        for copy in core_copies[j]:
            copy.wait_send()
    for group in (chip_copies, stat_copies, gather_copies, fwd_copies, mix_copies, out_copies):
        for copy in group.values():
            copy.wait_send()


def expected_embedding(part, active, embed_table, nx, nz, steps):
    rows, words = part.shape
    width = embed_table.shape[1]
    s = rows // (2 * nx) // steps
    block = 2 * nx * s
    far = max(nx - 1, 1)
    dma = pltpu.SemaphoreType.DMA
    return pl.pallas_call(
        functools.partial(mixed_kernel, nx, nz, steps),
        out_shape=jax.ShapeDtypeStruct((steps, block, width), jnp.bfloat16),
        in_specs=[
            pl.BlockSpec(memory_space=pl.ANY),
            pl.BlockSpec(memory_space=pltpu.VMEM),
            pl.BlockSpec(memory_space=pl.ANY),
        ],
        out_specs=pl.BlockSpec(memory_space=pltpu.VMEM),
        scratch_shapes=[
            pltpu.VMEM((steps, nx, s, words), jnp.float32),
            pltpu.VMEM((steps, nx, s, words), jnp.float32),
            pltpu.VMEM((steps, far, s, words), jnp.float32),
            pltpu.VMEM((steps, block, words), jnp.bfloat16),
            pltpu.VMEM((words, width), jnp.bfloat16),
            pltpu.VMEM((steps, block, width), jnp.bfloat16),
            pltpu.VMEM((steps, nz - 1, block // nz, width), jnp.bfloat16),
            pltpu.VMEM((steps, s, 128), jnp.float32),
            pltpu.VMEM((steps, nz - 1, s, 128), jnp.float32),
            dma,
            dma((steps, nx)), dma((steps, nx)), dma((steps, nx)),
            dma((steps, far)), dma((steps, far)),
            dma((steps, nz - 1)), dma((steps, nz - 1)),
            dma((steps,)), dma((steps,)),
            dma((steps, far)), dma((steps, far)),
            dma((steps, far)), dma((steps, far)),
            dma((steps, 2, nz - 1)), dma((steps, 2, nz - 1)),
            dma((steps, 2, nz - 1)), dma((steps, 2, nz - 1)),
        ],
        compiler_params=pltpu.CompilerParams(
            collective_id=0, has_side_effects=True, vmem_limit_bytes=VMEM_LIMIT
        ),
        name="expected_embedding",
    )(part, active, embed_table)


def qkv_kernel(nx, steps, part_ref, squares_ref, out_ref, core_buf, own_buf, chip_out, chip_in, squares_in,
               core_send, core_recv, own_sem, chip_send, chip_recv, sq_send, sq_recv):
    me, chip, core, partner, chip_at, peer = req_position(nx)
    own_rows = part_ref.shape[0] // (2 * nx)
    s = own_rows // steps
    n = 2 * nx
    others = [lax.rem(me + d, n) for d in range(1, n)]
    greet([{"req": other} for other in others])

    core_copies, own_copies = [], []
    for j in range(steps):
        core_copies.append([])
        own_copies.append([])
        for d in list(range(1, nx)) + [0]:
            there = pl.multiple_of(j * n * s + (chip_at(d) * 2 + 1 - core) * s, s)
            here = pl.multiple_of(j * n * s + (chip_at(d) * 2 + core) * s, s)
            copy = remote(part_ref.at[pl.ds(there, s)], core_buf.at[j, d], core_send.at[j, d],
                          core_recv.at[j, d], partner)
            local = pltpu.make_async_copy(part_ref.at[pl.ds(here, s)], own_buf.at[j, d], own_sem.at[j, d])
            copy.start()
            local.start()
            core_copies[j].append(copy)
            own_copies[j].append(local)
    sq_copies = []
    for i, other in enumerate(others):
        block = squares_ref.at[:, other]
        copy = remote(block, squares_in.at[i], sq_send.at[i], sq_recv.at[i], {"req": other})
        copy.start()
        sq_copies.append(copy)

    chip_copies = {}
    for j in range(steps):
        for i in range(nx):
            d = i + 1 if i < nx - 1 else 0
            own_copies[j][i].wait()
            core_copies[j][i].wait_recv()
            total = own_buf[j, d] + core_buf[j, d]
            if d > 0:
                chip_out[j, d - 1] = total.astype(chip_out.dtype)
                copy = remote(chip_out.at[j, d - 1], chip_in.at[j, d - 1], chip_send.at[j, d - 1],
                              chip_recv.at[j, d - 1], peer(d))
                copy.start()
                chip_copies[j, d] = copy
            else:
                own_buf[j, 0] = total
    squares = squares_ref[:, me]
    for i, copy in enumerate(sq_copies):
        copy.wait_recv()
        squares = squares + squares_in[i]
    inv_rms = lax.rsqrt(squares[:, :, 0:1] / D + 1e-05)
    for j in range(steps):
        total = own_buf[j, 0]
        for d in range(1, nx):
            chip_copies[j, d].wait_recv()
            total = total + chip_in[j, d - 1].astype(jnp.float32)
        out_ref[j * s : (j + 1) * s, :] = (total * inv_rms[j]).astype(out_ref.dtype)
    for j in range(steps):
        for copy in core_copies[j]:
            copy.wait_send()
    for copy in sq_copies + list(chip_copies.values()):
        copy.wait_send()


def scattered_qkv(part, squares, nx):
    rows, columns = part.shape
    steps = squares.shape[0]
    own = rows // (2 * nx)
    s = own // steps
    far = max(nx - 1, 1)
    dma = pltpu.SemaphoreType.DMA
    return pl.pallas_call(
        functools.partial(qkv_kernel, nx, steps),
        out_shape=jax.ShapeDtypeStruct((own, columns), jnp.bfloat16),
        in_specs=[pl.BlockSpec(memory_space=pl.ANY), pl.BlockSpec(memory_space=pltpu.VMEM)],
        out_specs=pl.BlockSpec(memory_space=pltpu.VMEM),
        scratch_shapes=[
            pltpu.VMEM((steps, nx, s, columns), jnp.float32),
            pltpu.VMEM((steps, nx, s, columns), jnp.float32),
            pltpu.VMEM((steps, far, s, columns), jnp.bfloat16),
            pltpu.VMEM((steps, far, s, columns), jnp.bfloat16),
            pltpu.VMEM((2 * nx - 1, steps, s, 128), jnp.float32),
            dma((steps, nx)), dma((steps, nx)), dma((steps, nx)),
            dma((steps, far)), dma((steps, far)),
            dma((2 * nx - 1,)), dma((2 * nx - 1,)),
        ],
        compiler_params=pltpu.CompilerParams(
            collective_id=2, has_side_effects=True, vmem_limit_bytes=VMEM_LIMIT
        ),
        name="qkv_sum",
    )(part, squares)


def on_device(nx, nz, last_states, head_weight, embed_table, norm_gain, qkv_weight, active, slot_request):
    rows = last_states.shape[0]
    state_rows = jnp.take(last_states, slot_request, axis=0)
    partial_logits = jnp.dot(state_rows, head_weight, preferred_element_type=jnp.float32)
    live = jnp.broadcast_to(active.astype(jnp.float32)[:, None], (rows, 128))
    own_rows = rows // (2 * nx)
    steps = 4
    while steps > 1 and (rows // steps // nz) % 16:
        steps //= 2
    s = own_rows // steps
    blocks = expected_embedding(partial_logits, live, embed_table, nx, nz, steps)
    widened = blocks.reshape(rows, -1).astype(jnp.float32)
    squares = jnp.broadcast_to(jnp.sum(widened * widened, axis=1)[:, None], (rows, 128))
    scaled = (widened * norm_gain.astype(jnp.float32)[None, :]).astype(jnp.bfloat16)
    partial_qkv = jnp.dot(scaled, qkv_weight, preferred_element_type=jnp.float32)
    qkv_out = scattered_qkv(partial_qkv, squares.reshape(steps, 2 * nx, s, 128), nx)
    soft_embed = blocks.reshape(steps, 2 * nx, s, -1).transpose(1, 0, 2, 3).reshape(rows, -1)
    return (soft_embed, qkv_out)


def solution(mesh):
    nx, nz = mesh.shape["req"] // 2, mesh.shape["vocab"]
    return jax.shard_map(
        functools.partial(on_device, nx, nz),
        mesh=mesh,
        in_specs=(
            P("groups", "req"),
            P("req", "vocab"),
            P("vocab", "req"),
            P("req"),
            P("req", "vocab"),
            P("groups"),
            P("groups"),
        ),
        out_specs=(P("groups", "req"), P(("groups", "req"), "vocab")),
        check_vma=False,
    )
```
